32 devices in a mesh: prow: 4 (over y, core), pcol: 8 (over z, x).
Axes of the slice: x: 2, y: 2, z: 4, core: 2. Of those that a mesh axis runs over, the one named last changes fastest.
Arguments:
- matrix: bfloat16 [14336, 4096], P('prow', 'pcol'), may hold values from -6 to 6
- u_inverse: float32 [2, 512, 512], replicated, may hold values from -0.02 to 0.2, as said below
- l_inverse: float32 [2, 512, 512], replicated, may hold values from -0.02 to 0.2, as said below
Outputs:
- factored: bfloat16 [14336, 4096], P('prow', 'pcol')
The draws below stay inside these ranges and needn't reach their ends.
Inputs may be any that keep to these rules, and one draw needn't show every extreme that they name: u_inverse[p] is upper triangular with positive diagonal. l_inverse[p] is lower triangular with positive diagonal.
All inputs are finite; a program needn't handle non-finite values.
Results may differ from the reference program's by a relative error of at most 0.008.
Values may be sent and summed in bfloat16 or wider, within the bound.
A program may use at most 64 MiB of HBM per device.

```python
import jax
import jax.numpy as jnp
from jax import lax

NB = 512
PANELS = 2
RB = 7
ORDER = 14336
WCOLS = 4096
N_PROW = 4


def draw_u_inverse(key, part):
    first, second = jax.random.split(jax.random.fold_in(key, 11))
    diagonal = jax.random.uniform(first, (PANELS, NB), jnp.float32, 0.1, 0.2)
    spread = jax.random.uniform(second, (PANELS, NB, NB), jnp.float32, -0.02, 0.02)
    return jnp.triu(spread, 1) + diagonal[:, :, None] * jnp.eye(NB, dtype=jnp.float32)[None]


def draw_l_inverse(key, part):
    first, second = jax.random.split(jax.random.fold_in(key, 23))
    diagonal = jax.random.uniform(first, (PANELS, NB), jnp.float32, 0.1, 0.2)
    spread = jax.random.uniform(second, (PANELS, NB, NB), jnp.float32, -0.02, 0.02)
    return jnp.tril(spread, -1) + diagonal[:, :, None] * jnp.eye(NB, dtype=jnp.float32)[None]


def block_scale(rng, extent, cuts, smallest, largest):
    loudness = 1.0
    for dim, blocks in cuts:
        steps = jax.random.uniform(jax.random.fold_in(jax.random.fold_in(rng, 6), dim), (blocks,), jnp.float32, smallest / len(cuts), largest / len(cuts))
        loudness = loudness * jnp.repeat(jnp.exp(steps), extent[dim] // blocks).reshape((-1,) + (1,) * (len(extent) - 1 - dim))
    return loudness


def scatter_about(stream_key, shape, scale, most, cuts=(), held_as=jnp.bfloat16):
    loudness = block_scale(stream_key, shape, cuts, -0.22, 0.18) if cuts else 1.0
    values = jax.random.normal(stream_key, shape, jnp.float32) * scale * loudness
    return jnp.minimum(jnp.maximum(values, -most), most).astype(held_as)


def setup_inputs(seed: int = 0) -> dict:
    arg_keys = jax.random.split(jax.random.key(seed), 4)
    matrix = scatter_about(arg_keys[0], (ORDER, WCOLS), 1.0, 6.0, ((0, 4), (1, 8)))
    u_inverse = draw_u_inverse(jax.random.fold_in(arg_keys[3], 71), 0)
    l_inverse = draw_l_inverse(jax.random.fold_in(arg_keys[3], 71), 0)
    return dict(matrix=matrix, u_inverse=u_inverse, l_inverse=l_inverse)


def reference(matrix, u_inverse, l_inverse):
    stored = jnp.arange(ORDER) // NB
    row_ids = (stored % RB) * N_PROW + stored // RB
    col_ids = jnp.arange(WCOLS) // NB
    current = matrix
    for panel_id in range(PANELS):
        start = panel_id * NB
        head_start = panel_id * RB * NB
        panel = current[:, start:start + NB].astype(jnp.float32)
        lower = jnp.dot(panel, u_inverse[panel_id], precision=lax.Precision.HIGHEST).astype(jnp.bfloat16)
        lower = jnp.where(row_ids[:, None] > panel_id, lower, jnp.zeros_like(lower))
        head = current[head_start:head_start + NB].astype(jnp.float32)
        upper = jnp.dot(l_inverse[panel_id], head, precision=lax.Precision.HIGHEST).astype(jnp.bfloat16)
        upper = jnp.where(col_ids[None, :] > panel_id, upper, jnp.zeros_like(upper))

        def refresh(pair, upper=upper):
            block, left = pair
            product = jnp.dot(left, upper, preferred_element_type=jnp.float32)
            return (block.astype(jnp.float32) - product).astype(jnp.bfloat16)

        blocks = lax.map(refresh, (current.reshape(ORDER // NB, NB, WCOLS), lower.reshape(ORDER // NB, NB, NB)))
        current = blocks.reshape(ORDER, WCOLS)
        current = current.at[:, start:start + NB].set(
            jnp.where(row_ids[:, None] > panel_id, lower, current[:, start:start + NB]))
        current = current.at[head_start:head_start + NB].set(
            jnp.where(col_ids[None, :] > panel_id, upper, current[head_start:head_start + NB]))
    return current
```

```python
import functools

import jax
import jax.numpy as jnp
from jax import lax
from jax.experimental import pallas as pl
from jax.experimental.pallas import tpu as pltpu
from jax.sharding import PartitionSpec as P

MESH = pl.DeviceIdType.MESH
BF = jnp.bfloat16
F32 = jnp.float32
PER_BLOCK = 8


def dot(a, b):
    return jnp.dot(a, b, preferred_element_type=F32)


def times_upper(a, u_ref, panel):
    half = a.shape[1] // 2
    left = sum(dot(a[:, :half], u_ref[panel, i, :half, :half]) for i in (2, 1, 0))
    right = sum(dot(a, u_ref[panel, i, :, half:]) for i in (2, 1, 0))
    return jnp.concatenate([left, right], 1).astype(BF)


def kernel(
    n_prow, n_pcol, width, m_ref, u_hbm, l_hbm, out_ref,
    own, buf, sbuf, uf, lf, us, ls, ucat, u1, lg1, cg1, low0, low1, cur, fresh, obuf,
    local_sem, recv, fwd, cross, sp_recv, sp_send, out_sem,
):
    rows = own.shape[0]
    chunk = width // PER_BLOCK
    chunks = rows // chunk
    half, blocks = width // 2, rows // width
    first = chunks - 4 * blocks
    prow, pcol = lax.axis_index("prow"), lax.axis_index("pcol")
    q, r = pcol % 2, prow % 2
    qx, rx = 1 - q, 1 - r
    pcol_x, prow_x = pcol + 1 - 2 * q, prow + 1 - 2 * r
    source, last = pcol < 2, pcol + 2 >= n_pcol
    top, bottom = prow < 2, prow + 2 >= n_prow
    special = pl.ds(rows, width)

    load_own = pltpu.make_async_copy(m_ref, own, local_sem.at[0])
    load_u = pltpu.make_async_copy(u_hbm, uf, local_sem.at[1])
    load_l = pltpu.make_async_copy(l_hbm, lf, local_sem.at[2])
    load_stream = pltpu.make_async_copy(m_ref, buf.at[q, pl.ds(0, rows)], local_sem.at[3])
    load_special = pltpu.make_async_copy(
        m_ref.at[pl.ds(0, width)], buf.at[q, special], local_sem.at[4]
    )
    load_head = pltpu.make_async_copy(m_ref.at[pl.ds(0, width)], sbuf.at[r], local_sem.at[5])
    source_special = source & (prow == qx)

    @pl.when(source)
    def _():
        load_stream.start()

    @pl.when(source_special)
    def _():
        load_special.start()

    @pl.when(top)
    def _():
        load_head.start()

    load_u.start()
    load_l.start()
    load_own.start()

    barrier = pltpu.get_barrier_semaphore()

    def greet(where):
        pl.semaphore_signal(barrier, inc=1, device_id=where, device_id_type=MESH)

    greet({"pcol": pcol_x})
    greet({"prow": prow_x})
    for ok, where in (
        (jnp.logical_not(source), {"pcol": pcol - 2}),
        (jnp.logical_not(last), {"pcol": pcol + 2}),
        (jnp.logical_not(top), {"prow": prow - 2}),
        (jnp.logical_not(bottom), {"prow": prow + 2}),
    ):
        pl.when(ok)(functools.partial(greet, where))
    absent = [jnp.where(ok, 1, 0) for ok in (source, last, top, bottom)]
    pl.semaphore_wait(barrier, 6 - sum(absent))

    def place(stream, k):
        shift = jnp.where((prow == 1 - stream) & (k < PER_BLOCK), rows, 0)
        at = pl.multiple_of(shift + k * chunk, chunk)
        return buf.at[stream, pl.ds(at, chunk)], (prow != stream) | (k >= PER_BLOCK)

    def stream_copy(stream, k, send_sem, where):
        ref, _ = place(stream, k)
        return pltpu.make_async_remote_copy(
            src_ref=ref, dst_ref=ref, send_sem=send_sem.at[k], recv_sem=recv.at[stream, k],
            device_id={"pcol": where}, device_id_type=MESH,
        )

    def send(k):
        @pl.when(jnp.logical_not(last))
        def _():
            stream_copy(q, k, fwd, pcol + 2).start()

        stream_copy(q, k, cross, pcol_x).start()

    def relay(k):
        @pl.when(jnp.logical_not(source) & place(q, k)[1])
        def _():
            stream_copy(q, k, fwd, pcol_x).wait_recv()
            send(k)

    def arrive(k):
        @pl.when(place(qx, k)[1])
        def _():
            stream_copy(qx, k, fwd, pcol_x).wait_recv()

    def loop(lo, hi, step):
        def one(k, carry):
            step(k)
            return carry

        lax.fori_loop(lo, hi, one, 0)

    def special_copy(which, across):
        ref = sbuf.at[r] if which == 0 else buf.at[rx, special]
        i = which + 2 * across
        return pltpu.make_async_remote_copy(
            src_ref=ref, dst_ref=ref, send_sem=sp_send.at[i], recv_sem=sp_recv.at[i],
            device_id={"prow": prow_x if across else prow + 2}, device_id_type=MESH,
        )

    def arrived_special(which, across):
        mine = rx if across else r
        ref = sbuf.at[mine] if which == 0 else buf.at[1 - mine, special]
        i = which + 2 * across
        pltpu.make_async_remote_copy(
            src_ref=ref, dst_ref=ref, send_sem=sp_send.at[i], recv_sem=sp_recv.at[i],
            device_id={"prow": prow_x}, device_id_type=MESH,
        ).wait_recv()

    def pass_special(which):
        @pl.when(jnp.logical_not(bottom))
        def _():
            special_copy(which, 0).start()

        special_copy(which, 1).start()

    @pl.when(top)
    def _():
        load_head.wait()
        pass_special(0)

    @pl.when(source_special)
    def _():
        load_special.wait()

    @pl.when(source)
    def _():
        load_stream.wait()
        loop(jnp.where(prow == q, PER_BLOCK, 0), chunks, send)

    load_u.wait()
    load_l.wait()
    load_own.wait()

    def split(src, dst, panel):
        rest = src[panel]
        for i in range(3):
            piece = rest.astype(BF)
            dst[panel, i] = piece
            rest = rest - piece.astype(F32)

    for n, (src, dst, panel) in enumerate(((lf, ls, 0), (uf, us, 0), (lf, ls, 1), (uf, us, 1))):
        split(src, dst, panel)
        relay(n)
    loop(4, PER_BLOCK, relay)

    @pl.when(top)
    def _():
        pl.when(q == r)(functools.partial(loop, 0, PER_BLOCK, arrive))
        pass_special(1)

    loop(PER_BLOCK, 2 * PER_BLOCK, relay)

    @pl.when(jnp.logical_not(top))
    def _():
        arrived_special(0, 0)
        pass_special(0)

    loop(2 * PER_BLOCK, first - 4, relay)

    @pl.when(jnp.logical_not(top))
    def _():
        arrived_special(1, 0)
        pass_special(1)

    loop(first - 4, first, relay)

    arrived_special(0, 1)
    arrived_special(1, 1)

    def lower_times(panel, value, out, at):
        upper = sum(dot(ls[panel, i, :half, :half], value[:half]) for i in (2, 1, 0))
        lower = sum(dot(ls[panel, i, half:], value) for i in (2, 1, 0))
        out[:half, at] = upper.astype(BF)
        out[half:, at] = lower.astype(BF)

    whole = slice(0, width)
    lower_times(0, buf[1, special], ucat, whole)
    relay(first)
    lower_times(0, sbuf[0], ucat, slice(width, 2 * width))
    relay(first + 1)
    lg1[...] = times_upper(buf[0, special], us, 0)
    relay(first + 2)
    cg1[...] = (sbuf[1].astype(F32) - dot(lg1[...], ucat[:, width:])).astype(BF)
    relay(first + 3)
    lower_times(1, cg1[...], u1, whole)

    def store(at, n, value, sem):
        obuf[pl.ds(at, n)] = value
        pltpu.make_async_copy(obuf.at[pl.ds(at, n)], out_ref.at[pl.ds(at, n)], sem).start()

    @pl.when(prow == 0)
    def _():
        store(0, width, jnp.where(pcol == 0, own[:width], ucat[:, width:]), out_sem.at[0])

    @pl.when(prow == 1)
    def _():
        value = jnp.where(pcol == 1, cg1[...], u1[...])
        store(0, width, jnp.where(pcol == 0, lg1[...], value), out_sem.at[0])

    def block(at, n, sem, between, active):
        at = pl.multiple_of(at, n)
        here, part = pl.ds(at, n), pl.ds(0, n)

        @pl.when(active)
        def _():
            low0[part] = times_upper(buf[0, here], us, 0)

        between(0)

        @pl.when(active)
        def _():
            a = dot(low0[part], ucat[...])
            cur[part] = (buf[1, here].astype(F32) - a[:, :width]).astype(BF)
            fresh[part] = (own[here].astype(F32) - a[:, width:]).astype(BF)

        between(1)

        @pl.when(active)
        def _():
            low1[part] = times_upper(cur[part], us, 1)

        between(2)

        @pl.when(active)
        def _():
            value = (fresh[part].astype(F32) - dot(low1[part], u1[...])).astype(BF)
            value = jnp.where(pcol == 1, low1[part], value)
            store(at, n, jnp.where(pcol == 0, low0[part], value), sem)

        between(3)

    def steps(b, slot):
        relay(first + 4 + b * 4 + slot)

    def one_block(b, carry):
        skip = (b == 0) & top

        @pl.when(jnp.logical_not(skip & (q == r)))
        def _():
            loop(b * PER_BLOCK, (b + 1) * PER_BLOCK, arrive)

        block(
            b * width, width, out_sem.at[b], functools.partial(steps, b), jnp.logical_not(skip)
        )
        return carry

    lax.fori_loop(0, blocks - 1, one_block, 0)
    for n in range(2):
        lo = (blocks - 1) * PER_BLOCK + n * (PER_BLOCK // 2)
        loop(lo, lo + PER_BLOCK // 2, arrive)
        block(lo * chunk, half, out_sem.at[blocks - 1 + n], lambda slot: None, True)

    for i in range(4):
        if i < 2:
            pl.when(jnp.logical_not(bottom))(special_copy(i, 0).wait_send)
        else:
            special_copy(i - 2, 1).wait_send()

    def sent(k):
        pl.when(jnp.logical_not(last))(lambda: stream_copy(q, k, fwd, pcol_x).wait_send())
        stream_copy(q, k, cross, pcol_x).wait_send()

    loop(jnp.where(prow == q, PER_BLOCK, 0), chunks, sent)

    def written(at, n, sem):
        pltpu.make_async_copy(obuf.at[pl.ds(at, n)], out_ref.at[pl.ds(at, n)], sem).wait()

    loop(0, blocks - 1, lambda b: written(pl.multiple_of(b * width, width), width, out_sem.at[b]))
    for n in range(2):
        written(rows - width + n * half, half, out_sem.at[blocks - 1 + n])


def body(n_prow, n_pcol, matrix, u_inverse, l_inverse):
    rows, width = matrix.shape
    chunks = rows // (width // PER_BLOCK)
    square = (width, width)
    dma = pltpu.SemaphoreType.DMA
    return pl.pallas_call(
        functools.partial(kernel, n_prow, n_pcol, width),
        out_shape=jax.ShapeDtypeStruct(matrix.shape, matrix.dtype),
        in_specs=[pl.BlockSpec(memory_space=pl.ANY)] * 3,
        out_specs=pl.BlockSpec(memory_space=pl.ANY),
        scratch_shapes=[
            pltpu.VMEM((rows, width), BF),
            pltpu.VMEM((2, rows + width, width), BF),
            pltpu.VMEM((2,) + square, BF),
            pltpu.VMEM((2,) + square, F32),
            pltpu.VMEM((2,) + square, F32),
            pltpu.VMEM((2, 3) + square, BF),
            pltpu.VMEM((2, 3) + square, BF),
            pltpu.VMEM((width, 2 * width), BF),
        ]
        + [pltpu.VMEM(square, BF)] * 7
        + [
            pltpu.VMEM((rows, width), BF),
            dma((6,)),
            dma((2, chunks)),
            dma((chunks,)),
            dma((chunks,)),
            dma((4,)),
            dma((4,)),
            dma((rows // width + 1,)),
        ],
        compiler_params=pltpu.CompilerParams(
            collective_id=0, has_side_effects=True, vmem_limit_bytes=60 * 1024 * 1024
        ),
    )(matrix, u_inverse, l_inverse)


def solution(mesh):
    run = functools.partial(body, mesh.shape["prow"], mesh.shape["pcol"])
    in_specs = (P("prow", "pcol"), P(), P())
    out_specs = P("prow", "pcol")
    return jax.shard_map(run, mesh=mesh, in_specs=in_specs, out_specs=out_specs, check_vma=False)
```

```python
import functools

import jax
import jax.numpy as jnp
from jax import lax
from jax.experimental import pallas as pl
from jax.experimental.pallas import tpu as pltpu
from jax.sharding import PartitionSpec as P

MESH = pl.DeviceIdType.MESH
BF = jnp.bfloat16
F32 = jnp.float32
PER_BLOCK = 16


def dot(a, b):
    return jnp.dot(a, b, preferred_element_type=F32)


def times_upper(a, u_ref, panel):
    half = a.shape[1] // 2
    left = sum(dot(a[:, :half], u_ref[panel, i, :half, :half]) for i in (2, 1, 0))
    right = sum(dot(a, u_ref[panel, i, :, half:]) for i in (2, 1, 0))
    return jnp.concatenate([left, right], 1).astype(BF)


def kernel(
    n_prow, n_pcol, width, m_ref, u_hbm, l_hbm, out_ref,
    own, buf, sbuf, uf, lf, us, ls, ucat, u1, lg1, cg1, low0, low1, cur, fresh, obuf,
    local_sem, recv, fwd, cross, sp_recv, sp_send, out_sem,
):
    rows = own.shape[0]
    chunk = width // PER_BLOCK
    chunks = rows // chunk
    half, blocks = width // 2, rows // width
    first = chunks - 4 * (2 * blocks - 1)
    prow, pcol = lax.axis_index("prow"), lax.axis_index("pcol")
    q, r = pcol % 2, prow % 2
    qx, rx = 1 - q, 1 - r
    pcol_x, prow_x = pcol + 1 - 2 * q, prow + 1 - 2 * r
    source, last = pcol < 2, pcol + 2 >= n_pcol
    top, bottom = prow < 2, prow + 2 >= n_prow
    special = pl.ds(rows, width)

    load_own = pltpu.make_async_copy(m_ref, own, local_sem.at[0])
    load_u = pltpu.make_async_copy(u_hbm, uf, local_sem.at[1])
    load_l = pltpu.make_async_copy(l_hbm, lf, local_sem.at[2])
    load_stream = pltpu.make_async_copy(m_ref, buf.at[q, pl.ds(0, rows)], local_sem.at[3])
    load_special = pltpu.make_async_copy(
        m_ref.at[pl.ds(0, width)], buf.at[q, special], local_sem.at[4]
    )
    load_head = pltpu.make_async_copy(m_ref.at[pl.ds(0, width)], sbuf.at[r], local_sem.at[5])
    source_special = source & (prow == qx)

    @pl.when(source)
    def _():
        load_stream.start()

    @pl.when(source_special)
    def _():
        load_special.start()

    @pl.when(top)
    def _():
        load_head.start()

    load_u.start()
    load_l.start()
    load_own.start()

    barrier = pltpu.get_barrier_semaphore()

    def greet(where):
        pl.semaphore_signal(barrier, inc=1, device_id=where, device_id_type=MESH)

    greet({"pcol": pcol_x})
    greet({"prow": prow_x})
    for ok, where in (
        (jnp.logical_not(source), {"pcol": pcol - 2}),
        (jnp.logical_not(last), {"pcol": pcol + 2}),
        (jnp.logical_not(top), {"prow": prow - 2}),
        (jnp.logical_not(bottom), {"prow": prow + 2}),
    ):
        pl.when(ok)(functools.partial(greet, where))
    absent = [jnp.where(ok, 1, 0) for ok in (source, last, top, bottom)]
    pl.semaphore_wait(barrier, 6 - sum(absent))

    def place(stream, k):
        shift = jnp.where((prow == 1 - stream) & (k < PER_BLOCK), rows, 0)
        at = pl.multiple_of(shift + k * chunk, chunk)
        return buf.at[stream, pl.ds(at, chunk)], (prow != stream) | (k >= PER_BLOCK)

    def stream_copy(stream, k, send_sem, where):
        ref, _ = place(stream, k)
        return pltpu.make_async_remote_copy(
            src_ref=ref, dst_ref=ref, send_sem=send_sem.at[k], recv_sem=recv.at[stream, k],
            device_id={"pcol": where}, device_id_type=MESH,
        )

    def send(k):
        @pl.when(jnp.logical_not(last))
        def _():
            stream_copy(q, k, fwd, pcol + 2).start()

        stream_copy(q, k, cross, pcol_x).start()

    ahead = jnp.where(prow == q, PER_BLOCK, 0)

    def relay(slot):
        k = slot + ahead

        @pl.when(jnp.logical_not(source) & (k < chunks))
        def _():
            stream_copy(q, k, fwd, pcol_x).wait_recv()
            send(k)

    def arrive(k):
        @pl.when(place(qx, k)[1])
        def _():
            stream_copy(qx, k, fwd, pcol_x).wait_recv()

    def loop(lo, hi, step):
        def one(k, carry):
            step(k)
            return carry

        lax.fori_loop(lo, hi, one, 0)

    def special_copy(which, across):
        ref = sbuf.at[r] if which == 0 else buf.at[rx, special]
        i = which + 2 * across
        return pltpu.make_async_remote_copy(
            src_ref=ref, dst_ref=ref, send_sem=sp_send.at[i], recv_sem=sp_recv.at[i],
            device_id={"prow": prow_x if across else prow + 2}, device_id_type=MESH,
        )

    def arrived_special(which, across):
        mine = rx if across else r
        ref = sbuf.at[mine] if which == 0 else buf.at[1 - mine, special]
        i = which + 2 * across
        pltpu.make_async_remote_copy(
            src_ref=ref, dst_ref=ref, send_sem=sp_send.at[i], recv_sem=sp_recv.at[i],
            device_id={"prow": prow_x}, device_id_type=MESH,
        ).wait_recv()

    def pass_special(which):
        @pl.when(jnp.logical_not(bottom))
        def _():
            special_copy(which, 0).start()

        special_copy(which, 1).start()

    @pl.when(top)
    def _():
        load_head.wait()
        pass_special(0)

    @pl.when(source_special)
    def _():
        load_special.wait()

    @pl.when(source)
    def _():
        load_stream.wait()
        loop(ahead, chunks, send)

    load_u.wait()
    load_l.wait()
    load_own.wait()

    def split(src, dst, panel):
        rest = src[panel]
        for i in range(3):
            piece = rest.astype(BF)
            dst[panel, i] = piece
            rest = rest - piece.astype(F32)

    for n, (src, dst, panel) in enumerate(((lf, ls, 0), (uf, us, 0), (lf, ls, 1), (uf, us, 1))):
        split(src, dst, panel)
        relay(n)
    loop(4, PER_BLOCK + 2, relay)

    @pl.when(top)
    def _():
        pl.when(q == r)(functools.partial(loop, 0, PER_BLOCK, arrive))
        pass_special(1)

    loop(PER_BLOCK + 2, 2 * PER_BLOCK, relay)

    @pl.when(jnp.logical_not(top))
    def _():
        arrived_special(0, 0)
        pass_special(0)

    loop(2 * PER_BLOCK, first - 16, relay)

    @pl.when(jnp.logical_not(top))
    def _():
        arrived_special(1, 0)
        pass_special(1)

    loop(first - 16, first - 8, relay)
    arrived_special(0, 1)
    arrived_special(1, 1)

    def lower_times(panel, value, out, at, slot):
        upper = sum(dot(ls[panel, i, :half, :half], value[:half]) for i in (2, 1, 0))
        out[:half, at] = upper.astype(BF)
        relay(slot)
        lower = sum(dot(ls[panel, i, half:], value) for i in (2, 1, 0))
        out[half:, at] = lower.astype(BF)
        relay(slot + 1)

    whole = slice(0, width)
    lower_times(0, buf[1, special], ucat, whole, first - 8)
    lower_times(0, sbuf[0], ucat, slice(width, 2 * width), first - 6)
    lg1[...] = times_upper(buf[0, special], us, 0)
    relay(first - 4)
    cg1[...] = (sbuf[1].astype(F32) - dot(lg1[...], ucat[:, width:])).astype(BF)
    relay(first - 3)
    lower_times(1, cg1[...], u1, whole, first - 2)

    def store(at, n, value, sem):
        obuf[pl.ds(at, n)] = value
        pltpu.make_async_copy(obuf.at[pl.ds(at, n)], out_ref.at[pl.ds(at, n)], sem).start()

    @pl.when(prow == 0)
    def _():
        store(0, width, jnp.where(pcol == 0, own[:width], ucat[:, width:]), out_sem.at[0])

    @pl.when(prow == 1)
    def _():
        value = jnp.where(pcol == 1, cg1[...], u1[...])
        store(0, width, jnp.where(pcol == 0, lg1[...], value), out_sem.at[0])

    def block(at, n, sem, between, active):
        at = pl.multiple_of(at, n)
        here, part = pl.ds(at, n), pl.ds(0, n)

        @pl.when(active)
        def _():
            low0[part] = times_upper(buf[0, here], us, 0)

        between(0)

        @pl.when(active)
        def _():
            a = dot(low0[part], ucat[...])
            cur[part] = (buf[1, here].astype(F32) - a[:, :width]).astype(BF)
            fresh[part] = (own[here].astype(F32) - a[:, width:]).astype(BF)

        between(1)

        @pl.when(active)
        def _():
            low1[part] = times_upper(cur[part], us, 1)

        between(2)

        @pl.when(active)
        def _():
            value = (fresh[part].astype(F32) - dot(low1[part], u1[...])).astype(BF)
            value = jnp.where(pcol == 1, low1[part], value)
            store(at, n, jnp.where(pcol == 0, low0[part], value), sem)

        between(3)

    tiles = 2 * blocks - 1

    def one_tile(t, carry):
        skip = (t < 2) & top

        @pl.when(jnp.logical_not(skip & (q == r)))
        def _():
            loop(t * (PER_BLOCK // 2), (t + 1) * (PER_BLOCK // 2), arrive)

        block(
            t * half,
            half,
            out_sem.at[1 + t],
            lambda slot: relay(first + 4 * t + slot),
            jnp.logical_not(skip),
        )
        return carry

    lax.fori_loop(0, tiles, one_tile, 0)
    quarter = half // 2
    for n in range(2):
        lo = tiles * (PER_BLOCK // 2) + n * (PER_BLOCK // 4)
        loop(lo, lo + PER_BLOCK // 4, arrive)
        block(lo * chunk, quarter, out_sem.at[1 + tiles + n], lambda slot: None, True)

    for i in range(4):
        if i < 2:
            pl.when(jnp.logical_not(bottom))(special_copy(i, 0).wait_send)
        else:
            special_copy(i - 2, 1).wait_send()

    def sent(k):
        pl.when(jnp.logical_not(last))(lambda: stream_copy(q, k, fwd, pcol_x).wait_send())
        stream_copy(q, k, cross, pcol_x).wait_send()

    loop(ahead, chunks, sent)

    def written(at, n, sem):
        pltpu.make_async_copy(obuf.at[pl.ds(at, n)], out_ref.at[pl.ds(at, n)], sem).wait()

    pl.when(top)(lambda: written(0, width, out_sem.at[0]))
    loop(
        jnp.where(top, 2, 0),
        tiles,
        lambda t: written(pl.multiple_of(t * half, half), half, out_sem.at[1 + t]),
    )
    for n in range(2):
        written(rows - half + n * quarter, quarter, out_sem.at[1 + tiles + n])


def body(n_prow, n_pcol, matrix, u_inverse, l_inverse):
    rows, width = matrix.shape
    chunks = rows // (width // PER_BLOCK)
    square = (width, width)
    dma = pltpu.SemaphoreType.DMA
    return pl.pallas_call(
        functools.partial(kernel, n_prow, n_pcol, width),
        out_shape=jax.ShapeDtypeStruct(matrix.shape, matrix.dtype),
        in_specs=[pl.BlockSpec(memory_space=pltpu.HBM)] * 3,
        out_specs=pl.BlockSpec(memory_space=pl.ANY),
        scratch_shapes=[
            pltpu.VMEM((rows, width), BF),
            pltpu.VMEM((2, rows + width, width), BF),
            pltpu.VMEM((2,) + square, BF),
            pltpu.VMEM((2,) + square, F32),
            pltpu.VMEM((2,) + square, F32),
            pltpu.VMEM((2, 3) + square, BF),
            pltpu.VMEM((2, 3) + square, BF),
            pltpu.VMEM((width, 2 * width), BF),
        ]
        + [pltpu.VMEM(square, BF)] * 7
        + [
            pltpu.VMEM((rows, width), BF),
            dma((6,)),
            dma((2, chunks)),
            dma((chunks,)),
            dma((chunks,)),
            dma((4,)),
            dma((4,)),
            dma((2 * rows // width + 2,)),
        ],
        compiler_params=pltpu.CompilerParams(
            collective_id=0, has_side_effects=True, vmem_limit_bytes=56 * 1024 * 1024
        ),
    )(matrix, u_inverse, l_inverse)


def solution(mesh):
    run = functools.partial(body, mesh.shape["prow"], mesh.shape["pcol"])
    in_specs = (P("prow", "pcol"), P(), P())
    out_specs = P("prow", "pcol")
    return jax.shard_map(run, mesh=mesh, in_specs=in_specs, out_specs=out_specs, check_vma=False)
```

```python
import functools

import jax
import jax.numpy as jnp
from jax import lax
from jax.experimental import pallas as pl
from jax.experimental.pallas import tpu as pltpu
from jax.sharding import PartitionSpec as P

MESH = pl.DeviceIdType.MESH
BF = jnp.bfloat16
F32 = jnp.float32
PER_BLOCK = 16


def dot(a, b):
    return jnp.dot(a, b, preferred_element_type=F32)


def times_upper(a, u_ref, panel):
    half = a.shape[1] // 2
    left = sum(dot(a[:, :half], u_ref[panel, i, :half, :half]) for i in (2, 1, 0))
    right = sum(dot(a, u_ref[panel, i, :, half:]) for i in (2, 1, 0))
    return jnp.concatenate([left, right], 1).astype(BF)


def kernel(
    n_prow, n_pcol, width, m_ref, u_hbm, l_hbm, out_ref,
    own, buf, sbuf, uf, lf, us, ls, ucat, u1, lg1, cg1, low0, low1, cur, fresh, obuf,
    local_sem, recv, fwd, cross, sp_recv, sp_send, out_sem,
):
    rows = own.shape[0]
    chunk = width // PER_BLOCK
    chunks = rows // chunk
    half, blocks = width // 2, rows // width
    first = chunks - 4 * (2 * blocks - 1)
    prow, pcol = lax.axis_index("prow"), lax.axis_index("pcol")
    q, r = pcol % 2, prow % 2
    qx, rx = 1 - q, 1 - r
    pcol_x, prow_x = pcol + 1 - 2 * q, prow + 1 - 2 * r
    source, last = pcol < 2, pcol + 2 >= n_pcol
    top, bottom = prow < 2, prow + 2 >= n_prow
    special = pl.ds(rows, width)

    load_own = pltpu.make_async_copy(m_ref, own, local_sem.at[0])
    load_u = pltpu.make_async_copy(u_hbm, uf, local_sem.at[1])
    load_l = pltpu.make_async_copy(l_hbm, lf, local_sem.at[2])
    load_stream = pltpu.make_async_copy(m_ref, buf.at[q, pl.ds(0, rows)], local_sem.at[3])
    load_special = pltpu.make_async_copy(
        m_ref.at[pl.ds(0, width)], buf.at[q, special], local_sem.at[4]
    )
    load_head = pltpu.make_async_copy(m_ref.at[pl.ds(0, width)], sbuf.at[r], local_sem.at[5])
    source_special = source & (prow == qx)

    @pl.when(source)
    def _():
        load_stream.start()

    @pl.when(source_special)
    def _():
        load_special.start()

    @pl.when(top)
    def _():
        load_head.start()

    load_u.start()
    load_l.start()
    load_own.start()

    barrier = pltpu.get_barrier_semaphore()

    def greet(where):
        pl.semaphore_signal(barrier, inc=1, device_id=where, device_id_type=MESH)

    greet({"pcol": pcol_x})
    greet({"prow": prow_x})
    for ok, where in (
        (jnp.logical_not(source), {"pcol": pcol - 2}),
        (jnp.logical_not(last), {"pcol": pcol + 2}),
        (jnp.logical_not(top), {"prow": prow - 2}),
        (jnp.logical_not(bottom), {"prow": prow + 2}),
    ):
        pl.when(ok)(functools.partial(greet, where))
    absent = [jnp.where(ok, 1, 0) for ok in (source, last, top, bottom)]
    pl.semaphore_wait(barrier, 6 - sum(absent))

    def place(stream, k):
        shift = jnp.where((prow == 1 - stream) & (k < PER_BLOCK), rows, 0)
        at = pl.multiple_of(shift + k * chunk, chunk)
        return buf.at[stream, pl.ds(at, chunk)], (prow != stream) | (k >= PER_BLOCK)

    def stream_copy(stream, k, send_sem, where, src=None):
        ref, _ = place(stream, k)
        return pltpu.make_async_remote_copy(
            src_ref=ref if src is None else src, dst_ref=ref, send_sem=send_sem.at[k], recv_sem=recv.at[stream, k],
            device_id={"pcol": where}, device_id_type=MESH,
        )

    def send(k, src=None):
        @pl.when(jnp.logical_not(last))
        def _():
            stream_copy(q, k, fwd, pcol + 2, src).start()

        stream_copy(q, k, cross, pcol_x, src).start()

    def send_own(k):
        send(k, m_ref.at[pl.ds(pl.multiple_of(k * chunk, chunk), chunk)])

    ahead = jnp.where(prow == q, PER_BLOCK, 0)

    def relay(slot):
        k = slot + ahead

        @pl.when(jnp.logical_not(source) & (k < chunks))
        def _():
            stream_copy(q, k, fwd, pcol_x).wait_recv()
            send(k)

    def arrive(k):
        @pl.when(place(qx, k)[1])
        def _():
            stream_copy(qx, k, fwd, pcol_x).wait_recv()

    def loop(lo, hi, step):
        def one(k, carry):
            step(k)
            return carry

        lax.fori_loop(lo, hi, one, 0)

    def special_copy(which, across):
        ref = sbuf.at[r] if which == 0 else buf.at[rx, special]
        i = which + 2 * across
        return pltpu.make_async_remote_copy(
            src_ref=ref, dst_ref=ref, send_sem=sp_send.at[i], recv_sem=sp_recv.at[i],
            device_id={"prow": prow_x if across else prow + 2}, device_id_type=MESH,
        )

    def arrived_special(which, across):
        mine = rx if across else r
        ref = sbuf.at[mine] if which == 0 else buf.at[1 - mine, special]
        i = which + 2 * across
        pltpu.make_async_remote_copy(
            src_ref=ref, dst_ref=ref, send_sem=sp_send.at[i], recv_sem=sp_recv.at[i],
            device_id={"prow": prow_x}, device_id_type=MESH,
        ).wait_recv()

    def pass_special(which):
        @pl.when(jnp.logical_not(bottom))
        def _():
            special_copy(which, 0).start()

        special_copy(which, 1).start()

    @pl.when(source)
    def _():
        loop(ahead, chunks, send_own)

    @pl.when(top)
    def _():
        load_head.wait()
        pass_special(0)

    @pl.when(source_special)
    def _():
        load_special.wait()

    loop(0, 6, relay)
    pl.when(source)(load_stream.wait)
    load_u.wait()
    load_l.wait()
    load_own.wait()

    def split(src, dst, panel):
        rest = src[panel]
        for i in range(3):
            piece = rest.astype(BF)
            dst[panel, i] = piece
            rest = rest - piece.astype(F32)

    for n, (src, dst, panel) in enumerate(((lf, ls, 0), (uf, us, 0), (lf, ls, 1), (uf, us, 1))):
        split(src, dst, panel)
        relay(6 + n)
    loop(10, PER_BLOCK + 2, relay)

    @pl.when(top)
    def _():
        pl.when(q == r)(functools.partial(loop, 0, PER_BLOCK, arrive))
        pass_special(1)

    loop(PER_BLOCK + 2, 2 * PER_BLOCK, relay)

    @pl.when(jnp.logical_not(top))
    def _():
        arrived_special(0, 0)
        pass_special(0)

    loop(2 * PER_BLOCK, first - 16, relay)

    @pl.when(jnp.logical_not(top))
    def _():
        arrived_special(1, 0)
        pass_special(1)

    loop(first - 16, first - 8, relay)
    arrived_special(0, 1)
    arrived_special(1, 1)

    def lower_times(panel, value, out, at, slot):
        upper = sum(dot(ls[panel, i, :half, :half], value[:half]) for i in (2, 1, 0))
        out[:half, at] = upper.astype(BF)
        relay(slot)
        lower = sum(dot(ls[panel, i, half:], value) for i in (2, 1, 0))
        out[half:, at] = lower.astype(BF)
        relay(slot + 1)

    whole = slice(0, width)
    lower_times(0, buf[1, special], ucat, whole, first - 8)
    lower_times(0, sbuf[0], ucat, slice(width, 2 * width), first - 6)
    lg1[...] = times_upper(buf[0, special], us, 0)
    relay(first - 4)
    cg1[...] = (sbuf[1].astype(F32) - dot(lg1[...], ucat[:, width:])).astype(BF)
    relay(first - 3)
    lower_times(1, cg1[...], u1, whole, first - 2)

    def store(at, n, value, sem):
        obuf[pl.ds(at, n)] = value
        pltpu.make_async_copy(obuf.at[pl.ds(at, n)], out_ref.at[pl.ds(at, n)], sem).start()

    @pl.when(prow == 0)
    def _():
        store(0, width, jnp.where(pcol == 0, own[:width], ucat[:, width:]), out_sem.at[0])

    @pl.when(prow == 1)
    def _():
        value = jnp.where(pcol == 1, cg1[...], u1[...])
        store(0, width, jnp.where(pcol == 0, lg1[...], value), out_sem.at[0])

    def block(at, n, sem, between, active):
        at = pl.multiple_of(at, n)
        here, part = pl.ds(at, n), pl.ds(0, n)

        @pl.when(active)
        def _():
            low0[part] = times_upper(buf[0, here], us, 0)

        between(0)

        @pl.when(active)
        def _():
            a = dot(low0[part], ucat[...])
            cur[part] = (buf[1, here].astype(F32) - a[:, :width]).astype(BF)
            fresh[part] = (own[here].astype(F32) - a[:, width:]).astype(BF)

        between(1)

        @pl.when(active)
        def _():
            low1[part] = times_upper(cur[part], us, 1)

        between(2)

        @pl.when(active)
        def _():
            value = (fresh[part].astype(F32) - dot(low1[part], u1[...])).astype(BF)
            value = jnp.where(pcol == 1, low1[part], value)
            store(at, n, jnp.where(pcol == 0, low0[part], value), sem)

        between(3)

    tiles = 2 * blocks - 1

    def one_tile(t, carry):
        skip = (t < 2) & top

        @pl.when(jnp.logical_not(skip & (q == r)))
        def _():
            loop(t * (PER_BLOCK // 2), (t + 1) * (PER_BLOCK // 2), arrive)

        block(
            t * half,
            half,
            out_sem.at[1 + t],
            lambda slot: relay(first + 4 * t + slot),
            jnp.logical_not(skip),
        )
        return carry

    lax.fori_loop(0, tiles, one_tile, 0)
    for i in range(4):
        if i < 2:
            pl.when(jnp.logical_not(bottom))(special_copy(i, 0).wait_send)
        else:
            special_copy(i - 2, 1).wait_send()

    def sent(k):
        pl.when(jnp.logical_not(last))(lambda: stream_copy(q, k, fwd, pcol_x).wait_send())
        stream_copy(q, k, cross, pcol_x).wait_send()

    late = chunks - PER_BLOCK // 2
    loop(ahead, late, sent)
    quarter = half // 2
    for n in range(2):
        lo = tiles * (PER_BLOCK // 2) + n * (PER_BLOCK // 4)
        loop(lo, lo + PER_BLOCK // 4, arrive)
        block(lo * chunk, quarter, out_sem.at[1 + tiles + n], lambda slot: None, True)

    loop(late, chunks, sent)

    def written(at, n, sem):
        pltpu.make_async_copy(obuf.at[pl.ds(at, n)], out_ref.at[pl.ds(at, n)], sem).wait()

    pl.when(top)(lambda: written(0, width, out_sem.at[0]))
    loop(
        jnp.where(top, 2, 0),
        tiles,
        lambda t: written(pl.multiple_of(t * half, half), half, out_sem.at[1 + t]),
    )
    for n in range(2):
        written(rows - half + n * quarter, quarter, out_sem.at[1 + tiles + n])


def body(n_prow, n_pcol, matrix, u_inverse, l_inverse):
    rows, width = matrix.shape
    chunks = rows // (width // PER_BLOCK)
    square = (width, width)
    dma = pltpu.SemaphoreType.DMA
    operands = [
        pltpu.with_memory_space_constraint(x, pltpu.HBM) for x in (matrix, u_inverse, l_inverse)
    ]
    return pl.pallas_call(
        functools.partial(kernel, n_prow, n_pcol, width),
        out_shape=jax.ShapeDtypeStruct(matrix.shape, matrix.dtype),
        in_specs=[pl.BlockSpec(memory_space=pltpu.HBM)] * 3,
        out_specs=pl.BlockSpec(memory_space=pl.ANY),
        scratch_shapes=[
            pltpu.VMEM((rows, width), BF),
            pltpu.VMEM((2, rows + width, width), BF),
            pltpu.VMEM((2,) + square, BF),
            pltpu.VMEM((2,) + square, F32),
            pltpu.VMEM((2,) + square, F32),
            pltpu.VMEM((2, 3) + square, BF),
            pltpu.VMEM((2, 3) + square, BF),
            pltpu.VMEM((width, 2 * width), BF),
        ]
        + [pltpu.VMEM(square, BF)] * 7
        + [
            pltpu.VMEM((rows, width), BF),
            dma((6,)),
            dma((2, chunks)),
            dma((chunks,)),
            dma((chunks,)),
            dma((4,)),
            dma((4,)),
            dma((2 * rows // width + 2,)),
        ],
        compiler_params=pltpu.CompilerParams(
            collective_id=0, has_side_effects=True, vmem_limit_bytes=46 * 1024 * 1024
        ),
    )(*operands)


def solution(mesh):
    run = functools.partial(body, mesh.shape["prow"], mesh.shape["pcol"])
    in_specs = (P("prow", "pcol"), P(), P())
    out_specs = P("prow", "pcol")
    return jax.shard_map(run, mesh=mesh, in_specs=in_specs, out_specs=out_specs, check_vma=False)
```

```python
import functools

import jax
import jax.numpy as jnp
from jax import lax
from jax.experimental import pallas as pl
from jax.experimental.pallas import tpu as pltpu
from jax.sharding import PartitionSpec as P

MESH = pl.DeviceIdType.MESH
BF = jnp.bfloat16
F32 = jnp.float32
PER_BLOCK = 16
PIECES = 2


def dot(a, b):
    return jnp.dot(a, b, preferred_element_type=F32)


def times_upper(a, u_ref, panel):
    half = a.shape[1] // 2
    left = sum(dot(a[:, :half], u_ref[panel, i, :half, :half]) for i in reversed(range(PIECES)))
    right = sum(dot(a, u_ref[panel, i, :, half:]) for i in reversed(range(PIECES)))
    return jnp.concatenate([left, right], 1).astype(BF)


def kernel(
    n_prow, n_pcol, width, m_ref, u_hbm, l_hbm, out_ref,
    own, buf, sbuf, uf, lf, us, ls, ucat, u1, lg1, cg1, low0, low1, cur, fresh, obuf,
    local_sem, recv, fwd, cross, sp_recv, sp_send, out_sem,
):
    rows = own.shape[0]
    chunk = width // PER_BLOCK
    chunks = rows // chunk
    half, blocks = width // 2, rows // width
    first = chunks - 4 * (2 * blocks - 1)
    prow, pcol = lax.axis_index("prow"), lax.axis_index("pcol")
    q, r = pcol % 2, prow % 2
    qx, rx = 1 - q, 1 - r
    pcol_x, prow_x = pcol + 1 - 2 * q, prow + 1 - 2 * r
    source, last = pcol < 2, pcol + 2 >= n_pcol
    top, bottom = prow < 2, prow + 2 >= n_prow
    special = pl.ds(rows, width)

    load_own = pltpu.make_async_copy(m_ref, own, local_sem.at[0])
    load_u = pltpu.make_async_copy(u_hbm, uf, local_sem.at[1])
    load_l = pltpu.make_async_copy(l_hbm, lf, local_sem.at[2])
    load_stream = pltpu.make_async_copy(m_ref, buf.at[q, pl.ds(0, rows)], local_sem.at[3])
    load_special = pltpu.make_async_copy(
        m_ref.at[pl.ds(0, width)], buf.at[q, special], local_sem.at[4]
    )
    load_head = pltpu.make_async_copy(m_ref.at[pl.ds(0, width)], sbuf.at[r], local_sem.at[5])
    source_special = source & (prow == qx)

    @pl.when(source)
    def _():
        load_stream.start()

    @pl.when(source_special)
    def _():
        load_special.start()

    @pl.when(top)
    def _():
        load_head.start()

    load_u.start()
    load_l.start()
    load_own.start()

    barrier = pltpu.get_barrier_semaphore()

    def greet(where):
        pl.semaphore_signal(barrier, inc=1, device_id=where, device_id_type=MESH)

    greet({"pcol": pcol_x})
    greet({"prow": prow_x})
    for ok, where in (
        (jnp.logical_not(source), {"pcol": pcol - 2}),
        (jnp.logical_not(last), {"pcol": pcol + 2}),
        (jnp.logical_not(top), {"prow": prow - 2}),
        (jnp.logical_not(bottom), {"prow": prow + 2}),
    ):
        pl.when(ok)(functools.partial(greet, where))
    absent = [jnp.where(ok, 1, 0) for ok in (source, last, top, bottom)]
    pl.semaphore_wait(barrier, 6 - sum(absent))

    def place(stream, k):
        shift = jnp.where((prow == 1 - stream) & (k < PER_BLOCK), rows, 0)
        at = pl.multiple_of(shift + k * chunk, chunk)
        return buf.at[stream, pl.ds(at, chunk)], (prow != stream) | (k >= PER_BLOCK)

    def stream_copy(stream, k, send_sem, where, src=None):
        ref, _ = place(stream, k)
        return pltpu.make_async_remote_copy(
            src_ref=ref if src is None else src, dst_ref=ref, send_sem=send_sem.at[k], recv_sem=recv.at[stream, k],
            device_id={"pcol": where}, device_id_type=MESH,
        )

    def send(k, src=None):
        @pl.when(jnp.logical_not(last))
        def _():
            stream_copy(q, k, fwd, pcol + 2, src).start()

        stream_copy(q, k, cross, pcol_x, src).start()

    def send_own(k):
        send(k, m_ref.at[pl.ds(pl.multiple_of(k * chunk, chunk), chunk)])

    ahead = jnp.where(prow == q, PER_BLOCK, 0)

    def relay(slot):
        k = slot + ahead

        @pl.when(jnp.logical_not(source) & (k < chunks))
        def _():
            stream_copy(q, k, fwd, pcol_x).wait_recv()
            send(k)

    def arrive(k):
        @pl.when(place(qx, k)[1])
        def _():
            stream_copy(qx, k, fwd, pcol_x).wait_recv()

    def loop(lo, hi, step):
        def one(k, carry):
            step(k)
            return carry

        lax.fori_loop(lo, hi, one, 0)

    def special_copy(which, across):
        ref = sbuf.at[r] if which == 0 else buf.at[rx, special]
        i = which + 2 * across
        return pltpu.make_async_remote_copy(
            src_ref=ref, dst_ref=ref, send_sem=sp_send.at[i], recv_sem=sp_recv.at[i],
            device_id={"prow": prow_x if across else prow + 2}, device_id_type=MESH,
        )

    def arrived_special(which, across):
        mine = rx if across else r
        ref = sbuf.at[mine] if which == 0 else buf.at[1 - mine, special]
        i = which + 2 * across
        pltpu.make_async_remote_copy(
            src_ref=ref, dst_ref=ref, send_sem=sp_send.at[i], recv_sem=sp_recv.at[i],
            device_id={"prow": prow_x}, device_id_type=MESH,
        ).wait_recv()

    def pass_special(which):
        @pl.when(jnp.logical_not(bottom))
        def _():
            special_copy(which, 0).start()

        special_copy(which, 1).start()

    @pl.when(source)
    def _():
        loop(ahead, chunks, send_own)

    @pl.when(top)
    def _():
        load_head.wait()
        pass_special(0)

    @pl.when(source_special)
    def _():
        load_special.wait()

    loop(0, 6, relay)
    pl.when(source)(load_stream.wait)
    load_u.wait()
    load_l.wait()
    load_own.wait()

    def split(src, dst, panel):
        rest = src[panel]
        for i in range(PIECES):
            piece = rest.astype(BF)
            dst[panel, i] = piece
            rest = rest - piece.astype(F32)

    for n, (src, dst, panel) in enumerate(((lf, ls, 0), (uf, us, 0), (lf, ls, 1), (uf, us, 1))):
        split(src, dst, panel)
        relay(6 + n)
    loop(10, PER_BLOCK + 2, relay)

    @pl.when(top)
    def _():
        pl.when(q == r)(functools.partial(loop, 0, PER_BLOCK, arrive))
        pass_special(1)

    loop(PER_BLOCK + 2, 2 * PER_BLOCK, relay)

    @pl.when(jnp.logical_not(top))
    def _():
        arrived_special(0, 0)
        pass_special(0)

    loop(2 * PER_BLOCK, first - 16, relay)

    @pl.when(jnp.logical_not(top))
    def _():
        arrived_special(1, 0)
        pass_special(1)

    loop(first - 16, first - 8, relay)
    arrived_special(0, 1)
    arrived_special(1, 1)

    def lower_times(panel, value, out, at, slot):
        upper = sum(dot(ls[panel, i, :half, :half], value[:half]) for i in reversed(range(PIECES)))
        out[:half, at] = upper.astype(BF)
        relay(slot)
        lower = sum(dot(ls[panel, i, half:], value) for i in reversed(range(PIECES)))
        out[half:, at] = lower.astype(BF)
        relay(slot + 1)

    whole = slice(0, width)
    lower_times(0, buf[1, special], ucat, whole, first - 8)
    lower_times(0, sbuf[0], ucat, slice(width, 2 * width), first - 6)
    lg1[...] = times_upper(buf[0, special], us, 0)
    relay(first - 4)
    cg1[...] = (sbuf[1].astype(F32) - dot(lg1[...], ucat[:, width:])).astype(BF)
    relay(first - 3)
    lower_times(1, cg1[...], u1, whole, first - 2)

    def store(at, n, value, sem):
        obuf[pl.ds(at, n)] = value
        pltpu.make_async_copy(obuf.at[pl.ds(at, n)], out_ref.at[pl.ds(at, n)], sem).start()

    @pl.when(prow == 0)
    def _():
        store(0, width, jnp.where(pcol == 0, own[:width], ucat[:, width:]), out_sem.at[0])

    @pl.when(prow == 1)
    def _():
        value = jnp.where(pcol == 1, cg1[...], u1[...])
        store(0, width, jnp.where(pcol == 0, lg1[...], value), out_sem.at[0])

    def block(at, n, sem, between, active):
        at = pl.multiple_of(at, n)
        here, part = pl.ds(at, n), pl.ds(0, n)

        @pl.when(active)
        def _():
            low0[part] = times_upper(buf[0, here], us, 0)

        between(0)

        @pl.when(active)
        def _():
            a = dot(low0[part], ucat[...])
            cur[part] = (buf[1, here].astype(F32) - a[:, :width]).astype(BF)
            fresh[part] = (own[here].astype(F32) - a[:, width:]).astype(BF)

        between(1)

        @pl.when(active)
        def _():
            low1[part] = times_upper(cur[part], us, 1)

        between(2)

        @pl.when(active)
        def _():
            value = (fresh[part].astype(F32) - dot(low1[part], u1[...])).astype(BF)
            value = jnp.where(pcol == 1, low1[part], value)
            store(at, n, jnp.where(pcol == 0, low0[part], value), sem)

        between(3)

    tiles = 2 * blocks - 1

    def one_tile(t, between):
        skip = (t < 2) & top

        @pl.when(jnp.logical_not(skip & (q == r)))
        def _():
            loop(t * (PER_BLOCK // 2), (t + 1) * (PER_BLOCK // 2), arrive)

        block(t * half, half, out_sem.at[1 + t], between, jnp.logical_not(skip))

    def nothing(slot):
        pass

    loop(0, tiles - 1, lambda t: one_tile(t, lambda slot: relay(first + 4 * t + slot)))
    loop(first + 4 * (tiles - 1), chunks, relay)
    one_tile(tiles - 1, nothing)

    quarter = half // 2

    def one_quarter(n):
        lo = tiles * (PER_BLOCK // 2) + n * (PER_BLOCK // 4)
        loop(lo, lo + PER_BLOCK // 4, arrive)
        block(lo * chunk, quarter, out_sem.at[1 + tiles + n], nothing, True)

    one_quarter(0)

    for i in range(4):
        if i < 2:
            pl.when(jnp.logical_not(bottom))(special_copy(i, 0).wait_send)
        else:
            special_copy(i - 2, 1).wait_send()

    def sent(k):
        pl.when(jnp.logical_not(last))(lambda: stream_copy(q, k, fwd, pcol_x).wait_send())
        stream_copy(q, k, cross, pcol_x).wait_send()

    late = chunks - PER_BLOCK // 2
    loop(ahead, late, sent)
    one_quarter(1)

    loop(late, chunks, sent)

    def written(at, n, sem):
        pltpu.make_async_copy(obuf.at[pl.ds(at, n)], out_ref.at[pl.ds(at, n)], sem).wait()

    pl.when(top)(lambda: written(0, width, out_sem.at[0]))
    loop(
        jnp.where(top, 2, 0),
        tiles,
        lambda t: written(pl.multiple_of(t * half, half), half, out_sem.at[1 + t]),
    )
    for n in range(2):
        written(rows - half + n * quarter, quarter, out_sem.at[1 + tiles + n])


def body(n_prow, n_pcol, matrix, u_inverse, l_inverse):
    rows, width = matrix.shape
    chunks = rows // (width // PER_BLOCK)
    square = (width, width)
    dma = pltpu.SemaphoreType.DMA
    operands = [
        pltpu.with_memory_space_constraint(x, pltpu.HBM) for x in (matrix, u_inverse, l_inverse)
    ]
    return pl.pallas_call(
        functools.partial(kernel, n_prow, n_pcol, width),
        out_shape=jax.ShapeDtypeStruct(matrix.shape, matrix.dtype),
        in_specs=[pl.BlockSpec(memory_space=pltpu.HBM)] * 3,
        out_specs=pl.BlockSpec(memory_space=pl.ANY),
        scratch_shapes=[
            pltpu.VMEM((rows, width), BF),
            pltpu.VMEM((2, rows + width, width), BF),
            pltpu.VMEM((2,) + square, BF),
            pltpu.VMEM((2,) + square, F32),
            pltpu.VMEM((2,) + square, F32),
            pltpu.VMEM((2, PIECES) + square, BF),
            pltpu.VMEM((2, PIECES) + square, BF),
            pltpu.VMEM((width, 2 * width), BF),
        ]
        + [pltpu.VMEM(square, BF)] * 7
        + [
            pltpu.VMEM((rows, width), BF),
            dma((6,)),
            dma((2, chunks)),
            dma((chunks,)),
            dma((chunks,)),
            dma((4,)),
            dma((4,)),
            dma((2 * rows // width + 2,)),
        ],
        compiler_params=pltpu.CompilerParams(
            collective_id=0, has_side_effects=True, vmem_limit_bytes=46 * 1024 * 1024
        ),
    )(*operands)


def solution(mesh):
    run = functools.partial(body, mesh.shape["prow"], mesh.shape["pcol"])
    in_specs = (P("prow", "pcol"), P(), P())
    out_specs = P("prow", "pcol")
    return jax.shard_map(run, mesh=mesh, in_specs=in_specs, out_specs=out_specs, check_vma=False)
```

```python
import functools

import jax
import jax.numpy as jnp
from jax import lax
from jax.experimental import pallas as pl
from jax.experimental.pallas import tpu as pltpu
from jax.sharding import PartitionSpec as P

MESH = pl.DeviceIdType.MESH
BF = jnp.bfloat16
F32 = jnp.float32
PER_BLOCK = 32
STEP = 2
PIECES = 3


def dot(a, b):
    return jnp.dot(a, b, preferred_element_type=F32)


def times_upper(a, u_ref, panel):
    half = a.shape[1] // 2
    left = sum(dot(a[:, :half], u_ref[panel, i, :half, :half]) for i in reversed(range(PIECES)))
    right = sum(dot(a, u_ref[panel, i, :, half:]) for i in reversed(range(PIECES)))
    return jnp.concatenate([left, right], 1).astype(BF)


def kernel(
    n_prow, n_pcol, width, m_ref, u_hbm, l_hbm, out_ref,
    own, buf, sbuf, uf, lf, us, ls, ucat, u1, lg1, cg1, low0, low1, cur, fresh, obuf,
    local_sem, recv, fwd, cross, sp_recv, sp_send, out_sem,
):
    rows = own.shape[0]
    chunk = width // PER_BLOCK
    chunks = rows // chunk
    half, blocks = width // 2, rows // width
    places = chunks // STEP
    first = places - 4 * (2 * blocks - 1)
    prow, pcol = lax.axis_index("prow"), lax.axis_index("pcol")
    q, r = pcol % 2, prow % 2
    qx, rx = 1 - q, 1 - r
    pcol_x, prow_x = pcol + 1 - 2 * q, prow + 1 - 2 * r
    source, last = pcol < 2, pcol + 2 >= n_pcol
    top, bottom = prow < 2, prow + 2 >= n_prow
    special = pl.ds(rows, width)

    load_own = pltpu.make_async_copy(m_ref, own, local_sem.at[0])
    load_u = pltpu.make_async_copy(u_hbm, uf, local_sem.at[1])
    load_l = pltpu.make_async_copy(l_hbm, lf, local_sem.at[2])
    load_stream = pltpu.make_async_copy(m_ref, buf.at[q, pl.ds(0, rows)], local_sem.at[3])
    load_special = pltpu.make_async_copy(
        m_ref.at[pl.ds(0, width)], buf.at[q, special], local_sem.at[4]
    )
    load_head = pltpu.make_async_copy(m_ref.at[pl.ds(0, width)], sbuf.at[r], local_sem.at[5])
    source_special = source & (prow == qx)

    @pl.when(source)
    def _():
        load_stream.start()

    @pl.when(source_special)
    def _():
        load_special.start()

    @pl.when(top)
    def _():
        load_head.start()

    load_u.start()
    load_l.start()
    load_own.start()

    barrier = pltpu.get_barrier_semaphore()

    def greet(where):
        pl.semaphore_signal(barrier, inc=1, device_id=where, device_id_type=MESH)

    greet({"pcol": pcol_x})
    greet({"prow": prow_x})
    for ok, where in (
        (jnp.logical_not(source), {"pcol": pcol - 2}),
        (jnp.logical_not(last), {"pcol": pcol + 2}),
        (jnp.logical_not(top), {"prow": prow - 2}),
        (jnp.logical_not(bottom), {"prow": prow + 2}),
    ):
        pl.when(ok)(functools.partial(greet, where))
    absent = [jnp.where(ok, 1, 0) for ok in (source, last, top, bottom)]
    pl.semaphore_wait(barrier, 6 - sum(absent))

    def place(stream, k):
        shift = jnp.where((prow == 1 - stream) & (k < PER_BLOCK), rows, 0)
        at = pl.multiple_of(shift + k * chunk, chunk)
        return buf.at[stream, pl.ds(at, chunk)], (prow != stream) | (k >= PER_BLOCK)

    def stream_copy(stream, k, send_sem, where, src=None):
        ref, _ = place(stream, k)
        return pltpu.make_async_remote_copy(
            src_ref=ref if src is None else src, dst_ref=ref, send_sem=send_sem.at[k], recv_sem=recv.at[stream, k],
            device_id={"pcol": where}, device_id_type=MESH,
        )

    def send(k, src=None):
        @pl.when(jnp.logical_not(last))
        def _():
            stream_copy(q, k, fwd, pcol + 2, src).start()

        stream_copy(q, k, cross, pcol_x, src).start()

    def send_own(k):
        send(k, m_ref.at[pl.ds(pl.multiple_of(k * chunk, chunk), chunk)])

    ahead = jnp.where(prow == q, PER_BLOCK, 0)

    def relay(slot):
        k = slot * STEP + ahead

        @pl.when(jnp.logical_not(source) & (k < chunks))
        def _():
            for i in range(STEP):
                stream_copy(q, k + i, fwd, pcol_x).wait_recv()
                send(k + i)

    def arrive(k):
        @pl.when(place(qx, k)[1])
        def _():
            stream_copy(qx, k, fwd, pcol_x).wait_recv()

    def loop(lo, hi, step):
        def one(k, carry):
            step(k)
            return carry

        lax.fori_loop(lo, hi, one, 0)

    def special_copy(which, across):
        ref = sbuf.at[r] if which == 0 else buf.at[rx, special]
        i = which + 2 * across
        return pltpu.make_async_remote_copy(
            src_ref=ref, dst_ref=ref, send_sem=sp_send.at[i], recv_sem=sp_recv.at[i],
            device_id={"prow": prow_x if across else prow + 2}, device_id_type=MESH,
        )

    def arrived_special(which, across):
        mine = rx if across else r
        ref = sbuf.at[mine] if which == 0 else buf.at[1 - mine, special]
        i = which + 2 * across
        pltpu.make_async_remote_copy(
            src_ref=ref, dst_ref=ref, send_sem=sp_send.at[i], recv_sem=sp_recv.at[i],
            device_id={"prow": prow_x}, device_id_type=MESH,
        ).wait_recv()

    def pass_special(which):
        @pl.when(jnp.logical_not(bottom))
        def _():
            special_copy(which, 0).start()

        special_copy(which, 1).start()

    @pl.when(source)
    def _():
        loop(ahead, chunks, send_own)

    @pl.when(top)
    def _():
        load_head.wait()
        pass_special(0)

    @pl.when(source_special)
    def _():
        load_special.wait()

    loop(0, 6, relay)
    pl.when(source)(load_stream.wait)
    load_u.wait()
    load_l.wait()
    load_own.wait()

    def split(src, dst, panel):
        rest = src[panel]
        for i in range(PIECES):
            piece = rest.astype(BF)
            dst[panel, i] = piece
            rest = rest - piece.astype(F32)

    for n, (src, dst, panel) in enumerate(((lf, ls, 0), (uf, us, 0), (lf, ls, 1), (uf, us, 1))):
        split(src, dst, panel)
        relay(6 + n)
    loop(10, PER_BLOCK // STEP + 2, relay)

    @pl.when(top)
    def _():
        pl.when(q == r)(functools.partial(loop, 0, PER_BLOCK, arrive))
        pass_special(1)

    loop(PER_BLOCK // STEP + 2, 2 * PER_BLOCK // STEP, relay)

    @pl.when(jnp.logical_not(top))
    def _():
        arrived_special(0, 0)
        pass_special(0)

    loop(2 * PER_BLOCK // STEP, first - 16, relay)

    @pl.when(jnp.logical_not(top))
    def _():
        arrived_special(1, 0)
        pass_special(1)

    loop(first - 16, first - 8, relay)
    arrived_special(0, 1)
    arrived_special(1, 1)

    def lower_times(panel, value, out, at, slot):
        upper = sum(dot(ls[panel, i, :half, :half], value[:half]) for i in reversed(range(PIECES)))
        out[:half, at] = upper.astype(BF)
        relay(slot)
        lower = sum(dot(ls[panel, i, half:], value) for i in reversed(range(PIECES)))
        out[half:, at] = lower.astype(BF)
        relay(slot + 1)

    whole = slice(0, width)
    lower_times(0, buf[1, special], ucat, whole, first - 8)
    lower_times(0, sbuf[0], ucat, slice(width, 2 * width), first - 6)
    lg1[...] = times_upper(buf[0, special], us, 0)
    relay(first - 4)
    cg1[...] = (sbuf[1].astype(F32) - dot(lg1[...], ucat[:, width:])).astype(BF)
    relay(first - 3)
    lower_times(1, cg1[...], u1, whole, first - 2)

    def store(at, n, value, sem):
        obuf[pl.ds(at, n)] = value
        pltpu.make_async_copy(obuf.at[pl.ds(at, n)], out_ref.at[pl.ds(at, n)], sem).start()

    @pl.when(prow == 0)
    def _():
        store(0, width, jnp.where(pcol == 0, own[:width], ucat[:, width:]), out_sem.at[0])

    @pl.when(prow == 1)
    def _():
        value = jnp.where(pcol == 1, cg1[...], u1[...])
        store(0, width, jnp.where(pcol == 0, lg1[...], value), out_sem.at[0])

    def block(at, n, sem, between, active):
        at = pl.multiple_of(at, n)
        here, part = pl.ds(at, n), pl.ds(0, n)

        @pl.when(active)
        def _():
            low0[part] = times_upper(buf[0, here], us, 0)

        between(0)

        @pl.when(active)
        def _():
            a = dot(low0[part], ucat[...])
            cur[part] = (buf[1, here].astype(F32) - a[:, :width]).astype(BF)
            fresh[part] = (own[here].astype(F32) - a[:, width:]).astype(BF)

        between(1)

        @pl.when(active)
        def _():
            low1[part] = times_upper(cur[part], us, 1)

        between(2)

        @pl.when(active)
        def _():
            value = (fresh[part].astype(F32) - dot(low1[part], u1[...])).astype(BF)
            value = jnp.where(pcol == 1, low1[part], value)
            store(at, n, jnp.where(pcol == 0, low0[part], value), sem)

        between(3)

    tiles = 2 * blocks - 1

    def one_tile(t, between):
        skip = (t < 2) & top

        @pl.when(jnp.logical_not(skip & (q == r)))
        def _():
            loop(t * (PER_BLOCK // 2), (t + 1) * (PER_BLOCK // 2), arrive)

        block(t * half, half, out_sem.at[1 + t], between, jnp.logical_not(skip))

    def nothing(slot):
        pass

    loop(0, tiles - 1, lambda t: one_tile(t, lambda slot: relay(first + 4 * t + slot)))
    loop(first + 4 * (tiles - 1), places, relay)
    one_tile(tiles - 1, nothing)

    quarter = half // 2

    def one_quarter(n):
        lo = tiles * (PER_BLOCK // 2) + n * (PER_BLOCK // 4)
        loop(lo, lo + PER_BLOCK // 4, arrive)
        block(lo * chunk, quarter, out_sem.at[1 + tiles + n], nothing, True)

    one_quarter(0)

    for i in range(4):
        if i < 2:
            pl.when(jnp.logical_not(bottom))(special_copy(i, 0).wait_send)
        else:
            special_copy(i - 2, 1).wait_send()

    def sent(k):
        pl.when(jnp.logical_not(last))(lambda: stream_copy(q, k, fwd, pcol_x).wait_send())
        stream_copy(q, k, cross, pcol_x).wait_send()

    late = chunks - PER_BLOCK // 2
    loop(ahead, late, sent)
    one_quarter(1)

    loop(late, chunks, sent)

    def written(at, n, sem):
        pltpu.make_async_copy(obuf.at[pl.ds(at, n)], out_ref.at[pl.ds(at, n)], sem).wait()

    pl.when(top)(lambda: written(0, width, out_sem.at[0]))
    loop(
        jnp.where(top, 2, 0),
        tiles,
        lambda t: written(pl.multiple_of(t * half, half), half, out_sem.at[1 + t]),
    )
    for n in range(2):
        written(rows - half + n * quarter, quarter, out_sem.at[1 + tiles + n])


def body(n_prow, n_pcol, matrix, u_inverse, l_inverse):
    rows, width = matrix.shape
    chunks = rows // (width // PER_BLOCK)
    square = (width, width)
    dma = pltpu.SemaphoreType.DMA
    operands = [
        pltpu.with_memory_space_constraint(x, pltpu.HBM) for x in (matrix, u_inverse, l_inverse)
    ]
    return pl.pallas_call(
        functools.partial(kernel, n_prow, n_pcol, width),
        out_shape=jax.ShapeDtypeStruct(matrix.shape, matrix.dtype),
        in_specs=[pl.BlockSpec(memory_space=pltpu.HBM)] * 3,
        out_specs=pl.BlockSpec(memory_space=pl.ANY),
        scratch_shapes=[
            pltpu.VMEM((rows, width), BF),
            pltpu.VMEM((2, rows + width, width), BF),
            pltpu.VMEM((2,) + square, BF),
            pltpu.VMEM((2,) + square, F32),
            pltpu.VMEM((2,) + square, F32),
            pltpu.VMEM((2, PIECES) + square, BF),
            pltpu.VMEM((2, PIECES) + square, BF),
            pltpu.VMEM((width, 2 * width), BF),
        ]
        + [pltpu.VMEM(square, BF)] * 7
        + [
            pltpu.VMEM((rows, width), BF),
            dma((6,)),
            dma((2, chunks)),
            dma((chunks,)),
            dma((chunks,)),
            dma((4,)),
            dma((4,)),
            dma((2 * rows // width + 2,)),
        ],
        compiler_params=pltpu.CompilerParams(
            collective_id=0, has_side_effects=True, vmem_limit_bytes=46 * 1024 * 1024
        ),
    )(*operands)


def solution(mesh):
    run = functools.partial(body, mesh.shape["prow"], mesh.shape["pcol"])
    in_specs = (P("prow", "pcol"), P(), P())
    out_specs = P("prow", "pcol")
    return jax.shard_map(run, mesh=mesh, in_specs=in_specs, out_specs=out_specs, check_vma=False)
```
